32 devices in a mesh: group: 4 (over x, core), seq: 8 (over z, y).
Axes of the slice: x: 2, y: 2, z: 4, core: 2. Of those that a mesh axis runs over, the one named last changes fastest.
Arguments:
- features: bfloat16 [16, 64, 16, 384], P('group', 'seq'), parts along dimension 0, may hold values from -6 to 6
- cotangent: bfloat16 [16, 64, 16, 192], P('group', 'seq'), parts along dimension 0, may hold values from -6 to 6
- conv_weight: bfloat16 [3, 3, 3, 384, 192], replicated, may hold values from -0.0625 to 0.0625
- patch_map: bfloat16 [1536, 4096], P('seq'), may hold values from -0.15625 to 0.15625
- qkv: bfloat16 [3, 4096, 4096], P(None, ('group', 'seq')), parts along dimension 1, may hold values from -122 to 122
Outputs:
- weight_grad: float32 [12, 3, 3, 384, 192], P('group'), parts along dimension 0
- grad_qkv: bfloat16 [3, 4096, 4096], P(None, ('group', 'seq')), parts along dimension 1
The draws below stay inside these ranges and needn't reach their ends.
There are 4 independent parts, one for each index of `group`. The reference program is written for one: setup_inputs(seed, part) draws one part's arguments, and reference() takes and returns one part's arrays. A program takes and returns all parts, laid end to end along the dimension named above; an argument that names none is the same for every part. Nothing has to cross between parts.
All inputs are finite; a program needn't handle non-finite values.
Results may differ from the reference program's by a relative error of at most 0.0075.
Values may be sent and summed in bfloat16 or wider, within the bound.
A program may use at most 128 MiB of HBM per device.

```python
import math
import jax
import jax.numpy as jnp
from jax import lax

CIN = 384
COUT = 192
HEADS = 32
FRAMES = 4
COLS = 16
HEIGHT = 64
PATCH = 1536
INNER = 4096
SEQUENCE = 1024


def draw_qkv(key, part):
    base = jnp.clip(jax.random.normal(key, (3, SEQUENCE, INNER), jnp.float32), -4.5, 4.5)
    return base.astype(jnp.bfloat16)


def block_levels(own_key, dims, split, least, high):
    factor_of, own = 1.0, jax.random.fold_in(own_key, 6)
    for axis_at, shards_of in split:
        steps = jnp.exp(jax.random.uniform(jax.random.fold_in(own, axis_at), (shards_of,), jnp.float32, least / len(split), high / len(split)))
        factor_of = factor_of * jnp.repeat(steps, dims[axis_at] // shards_of).reshape([-1 if axis == axis_at else 1 for axis in range(len(dims))])
    return factor_of


def gaussian(rng, shape, scale, reach, pieces=(), held_as=jnp.bfloat16):
    gain = block_levels(rng, shape, pieces, -0.22, 0.18) if pieces else 1.0
    values = jax.random.normal(rng, shape, jnp.float32) * scale * gain
    return jnp.minimum(jnp.maximum(values, -reach), reach).astype(held_as)


def setup_inputs(seed: int = 0, part: int = 0) -> dict:
    key_list = jax.random.split(jax.random.key(seed), 6)
    own_keys = jax.random.split(jax.random.fold_in(key_list[5], part), 6)
    return {
        "features": gaussian(own_keys[0], (FRAMES, HEIGHT, COLS, CIN), 1.0, 6.0, ((1, 8),)),
        "cotangent": gaussian(own_keys[1], (FRAMES, HEIGHT, COLS, COUT), 1.0, 6.0, ((1, 8),)),
        "conv_weight": gaussian(key_list[2], (3, 3, 3, CIN, COUT), (27 * CIN) ** -0.5, 0.0625),
        "patch_map": gaussian(key_list[3], (PATCH, INNER), PATCH ** -0.5, 0.15625, ((0, 8),)),
        "qkv": draw_qkv(jax.random.fold_in(jax.random.fold_in(key_list[5], part), 71), part),
    }


def attend_head(query, keys, values, grad_out):
    width = query.shape[1]
    scale = 1.0 / math.sqrt(width)
    scores = lax.dot_general(query, keys, (((1,), (1,)), ((), ())), preferred_element_type=jnp.float32) * scale
    top = lax.optimization_barrier(jnp.max(scores, axis=1, keepdims=True))
    expo = jnp.exp(scores - top)
    probs = expo / lax.optimization_barrier(jnp.sum(expo, axis=1, keepdims=True))
    dprob = lax.dot_general(grad_out, values, (((1,), (1,)), ((), ())), preferred_element_type=jnp.float32)
    delta = lax.optimization_barrier(jnp.sum(probs * dprob, axis=1, keepdims=True))
    dscore = (probs * (dprob - delta) * scale).astype(jnp.bfloat16)
    pround = probs.astype(jnp.bfloat16)
    dquery = jnp.dot(dscore, keys, preferred_element_type=jnp.float32).astype(jnp.bfloat16)
    dkeys = lax.dot_general(dscore, query, (((0,), (0,)), ((), ())), preferred_element_type=jnp.float32).astype(jnp.bfloat16)
    dvalues = lax.dot_general(pround, grad_out, (((0,), (0,)), ((), ())), preferred_element_type=jnp.float32).astype(jnp.bfloat16)
    return (dquery, dkeys, dvalues)

def reference(features, cotangent, conv_weight, patch_map, qkv):
    frames, height, cols, cin = features.shape
    cout = cotangent.shape[3]
    padded = jnp.pad(cotangent, ((0, 2), (1, 1), (1, 1), (0, 0)))
    flat_in = features.reshape(-1, cin)
    grad_in = jnp.zeros((frames * height * cols, cin), jnp.float32)
    taps = []
    for tap_t in range(3):
        for tap_h in range(3):
            for tap_w in range(3):
                shifted = padded[2 - tap_t:2 - tap_t + frames, 2 - tap_h:2 - tap_h + height, 2 - tap_w:2 - tap_w + cols]
                shifted = shifted.reshape(-1, cout)
                grad_in = grad_in + lax.dot_general(shifted, conv_weight[tap_t, tap_h, tap_w], (((1,), (1,)), ((), ())), preferred_element_type=jnp.float32)
                taps.append(lax.dot_general(flat_in, shifted, (((0,), (0,)), ((), ())), preferred_element_type=jnp.float32))
    weight_grad = jnp.stack(taps).reshape(3, 3, 3, cin, cout) * (1.0 / math.sqrt(frames * height * cols))
    grad_in = grad_in.reshape(frames, height // 2, 2, cols // 2, 2, cin).transpose(1, 0, 3, 2, 4, 5)
    patches = grad_in.reshape(-1, 4 * cin).astype(jnp.bfloat16)
    grad_out = jnp.dot(patches, patch_map, preferred_element_type=jnp.float32).astype(jnp.bfloat16)
    length = qkv.shape[1]
    heads_n = HEADS
    head_dim = qkv.shape[2] // heads_n
    stacked = qkv.reshape(3, length, heads_n, head_dim).transpose(0, 2, 1, 3)
    grads = grad_out.reshape(length, heads_n, head_dim).transpose(1, 0, 2)

    def one_head(packed):
        return attend_head(packed[0], packed[1], packed[2], packed[3])
    dquery, dkeys, dvalues = lax.map(one_head, (stacked[0], stacked[1], stacked[2], grads))
    result = jnp.stack([dquery, dkeys, dvalues]).transpose(0, 2, 1, 3).reshape(3, length, heads_n * head_dim)
    return (weight_grad, result)
```

```python
import math

import jax
import jax.numpy as jnp
from jax import lax
from jax.experimental import pallas as pl
from jax.experimental.pallas import tpu as pltpu
from jax.sharding import PartitionSpec as P

HEADS = 32
TILE = 32
LIMIT = 60 * 1024 * 1024
MESH = pl.DeviceIdType.MESH


def flops(count, moved):
    return pl.CostEstimate(flops=count, bytes_accessed=moved, transcendentals=0)


def grad_out_kernel(x_ref, w_ref, map_ref, out_ref, acc_ref):
    frames, span, wide = x_ref.shape[1], x_ref.shape[2], x_ref.shape[3]
    double = w_ref.shape[2]
    tap_h = pl.program_id(1)

    for side in range(2):
        for tap_t in (2, 1, 0):
            live = frames - 2 + tap_t
            rows = x_ref[side + 2 - tap_h, 2 - tap_t :].reshape(live * span, wide)
            part = lax.dot_general(
                rows, w_ref[tap_t, 0], (((1,), (1,)), ((), ())), preferred_element_type=jnp.float32
            )
            if tap_t == 2:

                @pl.when(tap_h == 0)
                def _():
                    acc_ref[side] = part

                @pl.when(tap_h > 0)
                def _():
                    acc_ref[side] += part

            else:
                acc_ref[side, : live * span] += part

    @pl.when(tap_h == 2)
    def _():
        wide_out = out_ref.shape[1]
        total = jnp.dot(
            acc_ref[0].astype(jnp.bfloat16), map_ref[:double], preferred_element_type=jnp.float32
        ) + jnp.dot(
            acc_ref[1].astype(jnp.bfloat16), map_ref[double:], preferred_element_type=jnp.float32
        )
        each = span // TILE
        total = total.reshape(frames, TILE, each, wide_out).transpose(1, 0, 2, 3)
        out_ref[...] = total.reshape(frames * span, wide_out).astype(jnp.bfloat16)


def weight_kernel(scale, blocks, feat_ref, x_ref, out_ref, turned_ref):
    frames, span, wide = x_ref.shape[1], x_ref.shape[2], x_ref.shape[3]
    double = feat_ref.shape[4]
    cin, cout = double // 2, wide // 4
    tap_h = pl.program_id(0)
    block = pl.program_id(1)

    def turn():
        for side in range(2):
            for frame in range(frames):
                turned_ref[side, :, frame * span : (frame + 1) * span] = (
                    feat_ref[:, side, frame].reshape(span, double).T
                )

    if blocks == 1:
        pl.when(tap_h == 0)(turn)
    else:
        turn()
    for tap_t in range(3):
        live = frames - 2 + tap_t
        prod = None
        for side in range(2):
            rows = x_ref[side + 2 - tap_h, 2 - tap_t :].reshape(live * span, wide)
            part = jnp.dot(
                turned_ref[side, :, : live * span], rows, preferred_element_type=jnp.float32
            )
            prod = part if prod is None else prod + part
        for tap_w in range(3):
            even = prod[:cin, cout * (2 - tap_w) : cout * (3 - tap_w)]
            odd = prod[cin:, cout * (3 - tap_w) : cout * (4 - tap_w)]
            value = (even + odd) * scale
            if blocks == 1:
                out_ref[tap_t, 0, tap_w] = value
            else:

                @pl.when(block == 0)
                def _():
                    out_ref[tap_t, 0, tap_w] = value

                @pl.when(block > 0)
                def _():
                    out_ref[tap_t, 0, tap_w] += value


def attention_kernel(step, qkv_ref, grad_ref, out_ref, dk_ref, dv_ref):
    shards, _, rows, width = qkv_ref.shape
    length = shards * rows
    scale = 1.0 / math.sqrt(width)
    keys = qkv_ref[:, 1].reshape(length, width)
    values = qkv_ref[:, 2].reshape(length, width)
    keys_t = keys.T
    span = step * rows

    def block(index, first):
        query = qkv_ref[pl.ds(index * step, step), 0].reshape(span, width)
        grads = grad_ref[pl.ds(pl.multiple_of(index * span, span), span), :]
        scores = lax.dot_general(
            keys, query, (((1,), (1,)), ((), ())), preferred_element_type=jnp.float32
        )
        top = jnp.max(scores, axis=0, keepdims=True)
        expo = jnp.exp((scores - top) * scale)
        probs = expo * (1.0 / jnp.sum(expo, axis=0, keepdims=True))
        dprob = lax.dot_general(
            values, grads, (((1,), (1,)), ((), ())), preferred_element_type=jnp.float32
        )
        delta = jnp.sum(probs * dprob, axis=0, keepdims=True)
        dscore = (probs * (dprob - delta)).astype(jnp.bfloat16)
        dquery = jnp.dot(keys_t, dscore, preferred_element_type=jnp.float32) * scale
        out_ref[pl.ds(index * step, step), 0] = (
            dquery.T.reshape(step, rows, width).astype(jnp.bfloat16)
        )
        part_k = jnp.dot(dscore, query, preferred_element_type=jnp.float32)
        part_v = jnp.dot(probs.astype(jnp.bfloat16), grads, preferred_element_type=jnp.float32)
        if first:
            dk_ref[...] = part_k
            dv_ref[...] = part_v
        else:
            dk_ref[...] += part_k
            dv_ref[...] += part_v

    count = shards // step
    if count <= 4:
        for index in range(count):
            block(index, index == 0)
    else:
        block(0, True)

        @pl.loop(1, count)
        def _(index):
            block(index, False)

    out_ref[:, 1] = (dk_ref[...] * scale).reshape(shards, rows, width).astype(jnp.bfloat16)
    out_ref[:, 2] = dv_ref[...].reshape(shards, rows, width).astype(jnp.bfloat16)


def per_device_general(features, cotangent, conv_weight, patch_map, qkv):
    frames, rows_here, cols, cin = features.shape
    cout = cotangent.shape[3]
    count = lax.axis_size("seq")
    parts = lax.axis_size("group")
    half, pairs = cols // 2, rows_here // 2
    pairs_all = pairs * count
    tokens_here, inner = qkv.shape[1], qkv.shape[2]
    length = tokens_here * count
    mine = inner // count
    head_dim = inner // HEADS

    cot = cotangent.reshape(frames, pairs, 2, half, 2 * cout).transpose(2, 0, 1, 3, 4)
    cot = lax.all_gather(cot.reshape(-1, 2 * cout), "seq", axis=0, tiled=True)
    sent = qkv.reshape(3, tokens_here, count, mine).transpose(2, 0, 1, 3)
    moved = lax.all_to_all(sent, "seq", split_axis=0, concat_axis=0, tiled=True)
    share = mine // parts
    depth = patch_map.shape[0]
    member = lax.axis_index("group")
    piece = lax.dynamic_index_in_dim(
        patch_map.reshape(depth, count, parts, share), member, axis=2, keepdims=False
    )
    piece = lax.all_to_all(
        piece.transpose(1, 0, 2), "seq", split_axis=0, concat_axis=0, tiled=True
    ).reshape(count * depth, share)
    columns = lax.all_gather(piece, "group", axis=0, tiled=False)
    columns = columns.transpose(1, 0, 2).reshape(count * depth, mine)
    feat = features.reshape(frames, pairs, 2, half, 2 * cin).transpose(2, 0, 1, 3, 4)
    feat = lax.all_gather(feat.reshape(-1, 2 * cin), "seq", axis=0, tiled=True)
    feat = feat.reshape(count, 2, frames, pairs * half, 2 * cin)

    full = cot.reshape(count, 2, frames, pairs, half, 2 * cout).transpose(1, 2, 0, 3, 4, 5)
    full = full.reshape(2, frames, pairs_all, half, 2 * cout)
    left = jnp.pad(full[:, :, :, :-1, cout:], ((0, 0), (0, 0), (0, 0), (1, 0), (0, 0)))
    right = jnp.pad(full[:, :, :, 1:, :cout], ((0, 0), (0, 0), (0, 0), (0, 1), (0, 0)))
    wide = jnp.concatenate([left, full, right], axis=-1)
    above = jnp.pad(wide[1][:, :-1], ((0, 0), (1, 0), (0, 0), (0, 0)))
    below = jnp.pad(wide[0][:, 1:], ((0, 0), (0, 1), (0, 0), (0, 0)))
    shifts = jnp.stack([above, wide[0], wide[1], below])
    shifts = shifts.reshape(4, frames, pairs_all * half, 4 * cout)

    taps = [conv_weight[:, :, tap_w] for tap_w in range(3)]
    blank = jnp.zeros_like(taps[0])
    big = jnp.concatenate(
        [
            jnp.concatenate([taps[2], taps[1], taps[0], blank], axis=-1),
            jnp.concatenate([blank, taps[2], taps[1], taps[0]], axis=-1),
        ],
        axis=2,
    )

    blocks = pairs_all // TILE
    span = TILE * half
    work = 2 * 9 * 3 * 2 * pairs_all * half * (2 * cin) * (4 * cout)
    x_block = pl.BlockSpec((4, frames, span, 4 * cout), lambda blk, tap: (0, 0, blk, 0))
    grad_out = pl.pallas_call(
        grad_out_kernel,
        grid=(blocks, 3),
        in_specs=[
            x_block,
            pl.BlockSpec((3, 1, 2 * cin, 4 * cout), lambda blk, tap: (0, tap, 0, 0)),
            pl.BlockSpec((count * depth, mine), lambda blk, tap: (0, 0)),
        ],
        out_specs=pl.BlockSpec((frames * span, mine), lambda blk, tap: (blk, 0)),
        out_shape=jax.ShapeDtypeStruct((length, mine), jnp.bfloat16),
        scratch_shapes=[pltpu.VMEM((2, frames * span, 2 * cin), jnp.float32)],
        compiler_params=pltpu.CompilerParams(vmem_limit_bytes=LIMIT),
        cost_estimate=flops(work, 20 << 20),
        name="grad_out",
    )(shifts, big, columns)

    step = max(1, 256 // tokens_here)
    head_block = pl.BlockSpec((count, 3, tokens_here, head_dim), lambda head: (0, 0, 0, head))
    heads_here = HEADS // count
    result = pl.pallas_call(
        lambda *refs: attention_kernel(step, *refs),
        grid=(heads_here,),
        in_specs=[head_block, pl.BlockSpec((length, head_dim), lambda head: (0, head))],
        out_specs=head_block,
        out_shape=jax.ShapeDtypeStruct((count, 3, tokens_here, mine), jnp.bfloat16),
        scratch_shapes=[pltpu.VMEM((length, head_dim), jnp.float32)] * 2,
        compiler_params=pltpu.CompilerParams(vmem_limit_bytes=LIMIT),
        cost_estimate=flops(heads_here * 20 * length * length * head_dim, 8 << 20),
        name="attention",
    )(moved, grad_out)

    shifts, result = lax.optimization_barrier((shifts, result))
    back = lax.all_to_all(result, "seq", split_axis=0, concat_axis=0, tiled=True)

    scale = 1.0 / math.sqrt(frames * rows_here * count * cols)
    shards = TILE // pairs
    weight_grad = pl.pallas_call(
        lambda *refs: weight_kernel(scale, blocks, *refs),
        grid=(3, blocks),
        in_specs=[
            pl.BlockSpec(
                (shards, 2, frames, pairs * half, 2 * cin), lambda tap, blk: (blk, 0, 0, 0, 0)
            ),
            pl.BlockSpec((4, frames, span, 4 * cout), lambda tap, blk: (0, 0, blk, 0)),
        ],
        out_specs=pl.BlockSpec((3, 1, 3, cin, cout), lambda tap, blk: (0, tap, 0, 0, 0)),
        out_shape=jax.ShapeDtypeStruct((3, 3, 3, cin, cout), jnp.float32),
        scratch_shapes=[pltpu.VMEM((2, 2 * cin, frames * span), jnp.bfloat16)],
        compiler_params=pltpu.CompilerParams(vmem_limit_bytes=LIMIT),
        cost_estimate=flops(work, 20 << 20),
        name="weight_grad",
    )(feat, shifts)
    back = back.transpose(1, 2, 0, 3).reshape(3, tokens_here, inner)
    return (weight_grad, back)


def fused_kernel(
    cot_ref, feat_ref, w_ref, map_ref, qkv_ref, wout_ref, back_ref,
    cot, feat, taps, big, cols, shifts, acc, grads, qkv_in, result, turned, dk, dv, stage,
    cot_send, cot_recv, feat_send, feat_recv, map_send, map_recv, share_send, share_recv,
    qkv_send, qkv_recv, back_send, back_recv, local, own, put,
):
    count = lax.axis_size("seq")
    parts = lax.axis_size("group")
    me = lax.axis_index("seq")
    member = lax.axis_index("group")
    lines = count // 2
    line, side_here = me // 2, lax.rem(me, 2)
    partner = me + 1 - 2 * side_here
    tokens, inner = qkv_ref.shape[1], qkv_ref.shape[2]
    mine = inner // count
    share = mine // parts
    depth = map_ref.shape[0]
    heads_here, head_dim = result.shape[0], result.shape[4]
    length = tokens * count
    frames = cot.shape[1]
    cin, cout = w_ref.shape[3], w_ref.shape[4]
    span = cot.shape[2]
    each = span // count

    barrier = pltpu.get_barrier_semaphore()
    for hop in range(1, count):
        pl.semaphore_signal(
            barrier, inc=1, device_id={"seq": lax.rem(me + hop, count)}, device_id_type=MESH
        )
    for hop in range(1, parts):
        pl.semaphore_signal(
            barrier, inc=1, device_id={"group": lax.rem(member + hop, parts)}, device_id_type=MESH
        )
    pl.semaphore_wait(barrier, count + parts - 2)

    def send(src, dst, sent, got, target):
        return pltpu.make_async_remote_copy(
            src_ref=src, dst_ref=dst, send_sem=sent, recv_sem=got, device_id=target,
            device_id_type=MESH,
        )

    class Gather:
        def __init__(self, source, full, sent, got, done):
            self.source, self.full, self.sent, self.got, self.done = source, full, sent, got, done

        def rows(self, owner):
            return self.full.at[:, :, pl.ds(pl.multiple_of(owner * each, each), each), :]

        def copy(self, slot, owner, target, first=False):
            src = self.source if first else self.rows(owner)
            return send(
                src, self.rows(owner), self.sent.at[slot], self.got.at[owner], {"seq": target}
            )

        def moves(self, hop):
            if hop == 0:
                return (
                    (line + 1 < lines, 0, me, me + 2),
                    (line > 0, 1, me, me - 2),
                    (None, 2, me, partner),
                )
            low, high = me - 2 * hop, me + 2 * hop
            base = 4 * hop - 1
            has_low, has_high = line >= hop, line + hop < lines
            return (
                (has_low & (line + 1 < lines), base, low, me + 2),
                (has_high & (line > 0), base + 1, high, me - 2),
                (has_low, base + 2, low, partner),
                (has_high, base + 3, high, partner),
            )

        def step(self, hop):
            if hop == 0:
                self.keep().start()
            else:
                for valid, owner in (
                    (line >= hop, me - 2 * hop),
                    (line + hop < lines, me + 2 * hop),
                ):

                    @pl.when(valid)
                    def _():
                        self.copy(0, owner, partner).wait_recv()

            for valid, slot, owner, target in self.moves(hop):
                copy = self.copy(slot, owner, target, first=hop == 0)
                if valid is None:
                    copy.start()
                else:
                    pl.when(valid)(copy.start)

        def keep(self):
            return pltpu.make_async_copy(self.source, self.rows(me), self.done)

        def finish(self):
            for other in range(lines):
                self.copy(0, 2 * other + 1 - side_here, partner).wait_recv()
            self.keep().wait()

        def drain(self):
            for hop in range(lines):
                for valid, slot, owner, target in self.moves(hop):
                    copy = self.copy(slot, owner, target, first=hop == 0)
                    if valid is None:
                        copy.wait_send()
                    else:
                        pl.when(valid)(copy.wait_send)

    gather_cot = Gather(cot_ref, cot, cot_send, cot_recv, own.at[0])
    gather_feat = Gather(feat_ref, feat, feat_send, feat_recv, own.at[1])

    def map_piece(target):
        return map_ref.at[:, pl.ds(pl.multiple_of(target * mine + member * share, share), share)]

    def map_slot(owner):
        return cols.at[
            pl.ds(pl.multiple_of(owner * depth, depth), depth),
            pl.ds(pl.multiple_of(member * share, share), share),
        ]

    def map_copy(hop):
        target = lax.rem(me + hop, count)
        return send(
            map_piece(target), map_slot(me), map_send.at[hop - 1], map_recv.at[hop - 1], {"seq": target}
        )

    def share_copy(hop):
        block = cols.at[:, pl.ds(pl.multiple_of(member * share, share), share)]
        return send(
            block, block, share_send.at[hop - 1], share_recv.at[hop - 1],
            {"group": lax.rem(member + hop, parts)},
        )

    def qkv_copy(head, hop):
        target = lax.rem(me + hop, count)
        return send(
            qkv_ref.at[:, :, pl.ds(pl.multiple_of(target * mine + head * head_dim, head_dim), head_dim)],
            qkv_in.at[head, me],
            qkv_send.at[head, hop - 1],
            qkv_recv.at[head, hop - 1],
            {"seq": target},
        )

    def qkv_keep(head):
        return pltpu.make_async_copy(
            qkv_ref.at[:, :, pl.ds(pl.multiple_of(me * mine + head * head_dim, head_dim), head_dim)],
            qkv_in.at[head, me],
            local.at[head],
        )

    def back_copy(head, hop):
        target = lax.rem(me + hop, count)
        place = back_ref.at[
            :, :, pl.ds(pl.multiple_of(me * mine + head * head_dim, head_dim), head_dim)
        ]
        return send(
            result.at[head, target], place, back_send.at[head, hop - 1],
            back_recv.at[head, hop - 1], {"seq": target},
        )

    def back_keep(head):
        place = back_ref.at[
            :, :, pl.ds(pl.multiple_of(me * mine + head * head_dim, head_dim), head_dim)
        ]
        return pltpu.make_async_copy(result.at[head, me], place, local.at[head])

    map_keep = pltpu.make_async_copy(map_piece(me), map_slot(me), own.at[2])
    taps_in = pltpu.make_async_copy(w_ref, taps, own.at[3])

    gather_cot.step(0)
    for hop in range(1, count):
        map_copy(hop).start()
    taps_in.start()
    map_keep.start()
    for head in range(heads_here):
        qkv_keep(head).start()
    for hop in range(1, lines):
        gather_cot.step(hop)

    def start_head(head):
        for hop in range(1, count):
            qkv_copy(head, hop).start()

    gather_feat.step(0)
    start_head(0)
    for hop in range(1, count):
        map_copy(hop).wait_recv()
    map_keep.wait()
    for hop in range(1, parts):
        share_copy(hop).start()

    taps_in.wait()
    gather_cot.finish()

    row = lax.broadcasted_iota(jnp.int32, (span, 2 * cout), 0)
    lane = lax.broadcasted_iota(jnp.int32, (span, 2 * cout), 1)
    half = span // TILE
    column = lax.rem(row, half)
    ahead = (lane < cout) & (column < half - 1)
    behind = (lane >= cout) & (column > 0)

    @pl.loop(0, 2 * frames)
    def _(index):
        side, frame = index // frames, lax.rem(index, frames)
        full = cot[side, frame]
        value = full.astype(jnp.float32)
        above = pltpu.roll(value, span - 1, 0)
        below = pltpu.roll(value, 1, 0)
        rest = jnp.where(ahead, above, jnp.where(behind, below, 0.0)).astype(jnp.bfloat16)
        shifts[side + 1, frame, :, : 2 * cout] = full
        shifts[side + 1, frame, :, 2 * cout :] = rest
        both = jnp.concatenate([value, rest.astype(jnp.float32)], axis=1)
        place = jnp.where(side == 0, 3, 0)
        gap = jnp.zeros((half, 4 * cout), jnp.float32)
        down = jnp.concatenate([gap, both[: span - half]], axis=0)
        up = jnp.concatenate([both[half:], gap], axis=0)
        shifts[place, frame] = jnp.where(side == 0, up, down).astype(jnp.bfloat16)

    acc[...] = jnp.zeros_like(acc)

    def convolve(tap_h):
        blank = jnp.zeros((cin, cout), jnp.bfloat16)
        for tap_t in range(3):
            first, middle, last = (taps[tap_t, tap_h, tap_w] for tap_w in range(3))
            big[tap_t, :cin] = jnp.concatenate([middle, first, blank, last], axis=1)
            big[tap_t, cin:] = jnp.concatenate([last, middle, first, blank], axis=1)

        @pl.loop(0, 2)
        def _(side):
            for tap_t in (2, 1, 0):
                live = frames - 2 + tap_t
                rows = shifts[side + 2 - tap_h, 2 - tap_t :].reshape(live * span, 4 * cout)
                acc[side, : live * span] += lax.dot_general(
                    rows, big[tap_t], (((1,), (1,)), ((), ())), preferred_element_type=jnp.float32
                )

    @pl.loop(0, 3)
    def _(tap_h):
        convolve(tap_h)
        for hop in range(1, 4):

            @pl.when(tap_h == hop - 1)
            def _():
                gather_feat.step(hop)
                start_head(hop)

    for hop in range(1, parts):
        share_copy(hop).wait_recv()
    total = jnp.dot(
        acc[0].astype(jnp.bfloat16), cols[: 2 * cin], preferred_element_type=jnp.float32
    ) + jnp.dot(acc[1].astype(jnp.bfloat16), cols[2 * cin :], preferred_element_type=jnp.float32)
    total = total.reshape(frames, span // half, half, mine).transpose(1, 0, 2, 3)
    total = total.reshape(length, mine).astype(jnp.bfloat16)
    for head in range(heads_here):
        grads[head] = total[:, head * head_dim : (head + 1) * head_dim]

    step = max(1, 256 // tokens)

    @pl.loop(0, heads_here)
    def _(head):
        qkv_keep(head).wait()
        for hop in range(1, count):
            qkv_copy(head, hop).wait_recv()
        attention_kernel(step, qkv_in.at[head], grads.at[head], result.at[head], dk, dv)
        for hop in range(1, count):
            back_copy(head, hop).start()
        back_keep(head).start()

    gather_feat.finish()
    for side in range(2):
        for frame in range(frames):
            turned[side, :, frame * span : (frame + 1) * span] = feat[side, frame].T

    scale = 1.0 / math.sqrt(2 * frames * span * 2)

    def out_copy(slot, tap_t, tap_h):
        return pltpu.make_async_copy(stage.at[slot, tap_t], wout_ref.at[tap_t, tap_h], put.at[slot, tap_t])

    @pl.loop(0, 3)
    def _(tap_h):
        slot = lax.rem(tap_h, 2)

        @pl.when(tap_h == 2)
        def _():
            for tap_t in range(3):
                out_copy(0, tap_t, 0).wait()

        for tap_t in range(3):
            live = frames - 2 + tap_t
            prod = None
            for side in range(2):
                rows = shifts[side + 2 - tap_h, 2 - tap_t :].reshape(live * span, 4 * cout)
                part = jnp.dot(
                    turned[side, :, : live * span], rows, preferred_element_type=jnp.float32
                )
                prod = part if prod is None else prod + part
            even, odd = prod[:cin], prod[cin:]
            for tap_w, (low, high) in enumerate(((1, 2), (0, 1), (3, 0))):
                value = even[:, low * cout : (low + 1) * cout] + odd[:, high * cout : (high + 1) * cout]
                stage[slot, tap_t, tap_w] = value * scale
            out_copy(slot, tap_t, tap_h).start()

    for tap_t in range(3):
        out_copy(1, tap_t, 1).wait()
        out_copy(0, tap_t, 2).wait()

    gather_cot.drain()
    gather_feat.drain()
    for hop in range(1, count):
        map_copy(hop).wait_send()
    for hop in range(1, parts):
        share_copy(hop).wait_send()

    @pl.loop(0, heads_here)
    def _(head):
        for hop in range(1, count):
            qkv_copy(head, hop).wait_send()
            back_copy(head, hop).wait_send()
        for hop in range(1, count):
            back_copy(head, hop).wait_recv()
        back_keep(head).wait()


def per_device(features, cotangent, conv_weight, patch_map, qkv):
    frames, rows_here, cols, cin = features.shape
    cout = cotangent.shape[3]
    count, parts = lax.axis_size("seq"), lax.axis_size("group")
    half, pairs = cols // 2, rows_here // 2
    span = pairs * half * count
    tokens, inner = qkv.shape[1], qkv.shape[2]
    mine, head_dim = inner // count, inner // HEADS
    heads_here = HEADS // count
    depth = patch_map.shape[0]
    fits = count == 8 and heads_here == 4 and (mine // parts) % 128 == 0
    if not (fits and half == 8 and span == TILE * half):
        return per_device_general(features, cotangent, conv_weight, patch_map, qkv)

    def paired(value, wide):
        value = value.reshape(frames, pairs, 2, half, 2 * wide).transpose(2, 0, 1, 3, 4)
        return value.reshape(2, frames, pairs * half, 2 * wide)

    half_type, dma = jnp.bfloat16, pltpu.SemaphoreType.DMA
    whole = pl.BlockSpec(memory_space=pl.ANY)
    moves = 4 * (count // 2) - 1
    return pl.pallas_call(
        fused_kernel,
        in_specs=[whole] * 5,
        out_specs=[whole] * 2,
        out_shape=[
            jax.ShapeDtypeStruct((3, 3, 3, cin, cout), jnp.float32),
            jax.ShapeDtypeStruct((3, tokens, inner), half_type),
        ],
        scratch_shapes=[
            pltpu.VMEM((2, frames, span, 2 * cout), half_type),
            pltpu.VMEM((2, frames, span, 2 * cin), half_type),
            pltpu.VMEM((3, 3, 3, cin, cout), half_type),
            pltpu.VMEM((3, 2 * cin, 4 * cout), half_type),
            pltpu.VMEM((count * depth, mine), half_type),
            pltpu.VMEM((4, frames, span, 4 * cout), half_type),
            pltpu.VMEM((2, frames * span, 2 * cin), jnp.float32),
            pltpu.VMEM((heads_here, tokens * count, head_dim), half_type),
            pltpu.VMEM((heads_here, count, 3, tokens, head_dim), half_type),
            pltpu.VMEM((heads_here, count, 3, tokens, head_dim), half_type),
            pltpu.VMEM((2, 2 * cin, frames * span), half_type),
            pltpu.VMEM((tokens * count, head_dim), jnp.float32),
            pltpu.VMEM((tokens * count, head_dim), jnp.float32),
            pltpu.VMEM((2, 3, 3, cin, cout), jnp.float32),
            dma((moves,)), dma((count,)), dma((moves,)), dma((count,)),
            dma((count - 1,)), dma((count - 1,)), dma((parts - 1,)), dma((parts - 1,)),
            dma((heads_here, count - 1)), dma((heads_here, count - 1)),
            dma((heads_here, count - 1)), dma((heads_here, count - 1)),
            dma((heads_here,)), dma((4,)), dma((2, 3)),
        ],
        compiler_params=pltpu.CompilerParams(
            collective_id=0, has_side_effects=True, vmem_limit_bytes=LIMIT
        ),
        name="fused",
    )(paired(cotangent, cout), paired(features, cin), conv_weight, patch_map, qkv)


def solution(mesh):
    placed = (
        P("group", "seq", None, None),
        P("group", "seq", None, None),
        P(),
        P("seq", None),
        P(None, ("group", "seq"), None),
    )
    return jax.shard_map(
        per_device,
        mesh=mesh,
        in_specs=placed,
        out_specs=(P("group", None, None, None, None), P(None, ("group", "seq"), None)),
        check_vma=False,
    )
```

```python
import math

import jax
import jax.numpy as jnp
from jax import lax
from jax.experimental import pallas as pl
from jax.experimental.pallas import tpu as pltpu
from jax.sharding import PartitionSpec as P

HEADS = 32
TILE = 32
LIMIT = 60 * 1024 * 1024
MESH = pl.DeviceIdType.MESH


def flops(count, moved):
    return pl.CostEstimate(flops=count, bytes_accessed=moved, transcendentals=0)


def grad_out_kernel(x_ref, w_ref, map_ref, out_ref, acc_ref):
    frames, span, wide = x_ref.shape[1], x_ref.shape[2], x_ref.shape[3]
    double = w_ref.shape[2]
    tap_h = pl.program_id(1)

    for side in range(2):
        for tap_t in (2, 1, 0):
            live = frames - 2 + tap_t
            rows = x_ref[side + 2 - tap_h, 2 - tap_t :].reshape(live * span, wide)
            part = lax.dot_general(
                rows, w_ref[tap_t, 0], (((1,), (1,)), ((), ())), preferred_element_type=jnp.float32
            )
            if tap_t == 2:

                @pl.when(tap_h == 0)
                def _():
                    acc_ref[side] = part

                @pl.when(tap_h > 0)
                def _():
                    acc_ref[side] += part

            else:
                acc_ref[side, : live * span] += part

    @pl.when(tap_h == 2)
    def _():
        wide_out = out_ref.shape[1]
        total = jnp.dot(
            acc_ref[0].astype(jnp.bfloat16), map_ref[:double], preferred_element_type=jnp.float32
        ) + jnp.dot(
            acc_ref[1].astype(jnp.bfloat16), map_ref[double:], preferred_element_type=jnp.float32
        )
        each = span // TILE
        total = total.reshape(frames, TILE, each, wide_out).transpose(1, 0, 2, 3)
        out_ref[...] = total.reshape(frames * span, wide_out).astype(jnp.bfloat16)


def weight_kernel(scale, blocks, feat_ref, x_ref, out_ref, turned_ref):
    frames, span, wide = x_ref.shape[1], x_ref.shape[2], x_ref.shape[3]
    double = feat_ref.shape[4]
    cin, cout = double // 2, wide // 4
    tap_h = pl.program_id(0)
    block = pl.program_id(1)

    def turn():
        for side in range(2):
            for frame in range(frames):
                turned_ref[side, :, frame * span : (frame + 1) * span] = (
                    feat_ref[:, side, frame].reshape(span, double).T
                )

    if blocks == 1:
        pl.when(tap_h == 0)(turn)
    else:
        turn()
    for tap_t in range(3):
        live = frames - 2 + tap_t
        prod = None
        for side in range(2):
            rows = x_ref[side + 2 - tap_h, 2 - tap_t :].reshape(live * span, wide)
            part = jnp.dot(
                turned_ref[side, :, : live * span], rows, preferred_element_type=jnp.float32
            )
            prod = part if prod is None else prod + part
        for tap_w in range(3):
            even = prod[:cin, cout * (2 - tap_w) : cout * (3 - tap_w)]
            odd = prod[cin:, cout * (3 - tap_w) : cout * (4 - tap_w)]
            value = (even + odd) * scale
            if blocks == 1:
                out_ref[tap_t, 0, tap_w] = value
            else:

                @pl.when(block == 0)
                def _():
                    out_ref[tap_t, 0, tap_w] = value

                @pl.when(block > 0)
                def _():
                    out_ref[tap_t, 0, tap_w] += value


def attention_kernel(step, qkv_ref, grad_ref, out_ref, dk_ref, dv_ref):
    shards, _, rows, width = qkv_ref.shape
    length = shards * rows
    scale = 1.0 / math.sqrt(width)
    keys = qkv_ref[:, 1].reshape(length, width)
    values = qkv_ref[:, 2].reshape(length, width)
    keys_t = keys.T
    span = step * rows

    def block(index, first):
        query = qkv_ref[pl.ds(index * step, step), 0].reshape(span, width)
        grads = grad_ref[pl.ds(pl.multiple_of(index * span, span), span), :]
        scores = lax.dot_general(
            keys, query, (((1,), (1,)), ((), ())), preferred_element_type=jnp.float32
        )
        top = jnp.max(scores, axis=0, keepdims=True)
        expo = jnp.exp((scores - top) * scale)
        probs = expo * (1.0 / jnp.sum(expo, axis=0, keepdims=True))
        dprob = lax.dot_general(
            values, grads, (((1,), (1,)), ((), ())), preferred_element_type=jnp.float32
        )
        delta = jnp.sum(probs * dprob, axis=0, keepdims=True)
        dscore = (probs * (dprob - delta)).astype(jnp.bfloat16)
        dquery = jnp.dot(keys_t, dscore, preferred_element_type=jnp.float32) * scale
        out_ref[pl.ds(index * step, step), 0] = (
            dquery.T.reshape(step, rows, width).astype(jnp.bfloat16)
        )
        part_k = jnp.dot(dscore, query, preferred_element_type=jnp.float32)
        part_v = jnp.dot(probs.astype(jnp.bfloat16), grads, preferred_element_type=jnp.float32)
        if first:
            dk_ref[...] = part_k
            dv_ref[...] = part_v
        else:
            dk_ref[...] += part_k
            dv_ref[...] += part_v

    count = shards // step
    if count <= 4:
        for index in range(count):
            block(index, index == 0)
    else:
        block(0, True)

        @pl.loop(1, count)
        def _(index):
            block(index, False)

    out_ref[:, 1] = (dk_ref[...] * scale).reshape(shards, rows, width).astype(jnp.bfloat16)
    out_ref[:, 2] = dv_ref[...].reshape(shards, rows, width).astype(jnp.bfloat16)


def per_device_general(features, cotangent, conv_weight, patch_map, qkv):
    frames, rows_here, cols, cin = features.shape
    cout = cotangent.shape[3]
    count = lax.axis_size("seq")
    parts = lax.axis_size("group")
    half, pairs = cols // 2, rows_here // 2
    pairs_all = pairs * count
    tokens_here, inner = qkv.shape[1], qkv.shape[2]
    length = tokens_here * count
    mine = inner // count
    head_dim = inner // HEADS

    cot = cotangent.reshape(frames, pairs, 2, half, 2 * cout).transpose(2, 0, 1, 3, 4)
    cot = lax.all_gather(cot.reshape(-1, 2 * cout), "seq", axis=0, tiled=True)
    sent = qkv.reshape(3, tokens_here, count, mine).transpose(2, 0, 1, 3)
    moved = lax.all_to_all(sent, "seq", split_axis=0, concat_axis=0, tiled=True)
    share = mine // parts
    depth = patch_map.shape[0]
    member = lax.axis_index("group")
    piece = lax.dynamic_index_in_dim(
        patch_map.reshape(depth, count, parts, share), member, axis=2, keepdims=False
    )
    piece = lax.all_to_all(
        piece.transpose(1, 0, 2), "seq", split_axis=0, concat_axis=0, tiled=True
    ).reshape(count * depth, share)
    columns = lax.all_gather(piece, "group", axis=0, tiled=False)
    columns = columns.transpose(1, 0, 2).reshape(count * depth, mine)
    feat = features.reshape(frames, pairs, 2, half, 2 * cin).transpose(2, 0, 1, 3, 4)
    feat = lax.all_gather(feat.reshape(-1, 2 * cin), "seq", axis=0, tiled=True)
    feat = feat.reshape(count, 2, frames, pairs * half, 2 * cin)

    full = cot.reshape(count, 2, frames, pairs, half, 2 * cout).transpose(1, 2, 0, 3, 4, 5)
    full = full.reshape(2, frames, pairs_all, half, 2 * cout)
    left = jnp.pad(full[:, :, :, :-1, cout:], ((0, 0), (0, 0), (0, 0), (1, 0), (0, 0)))
    right = jnp.pad(full[:, :, :, 1:, :cout], ((0, 0), (0, 0), (0, 0), (0, 1), (0, 0)))
    wide = jnp.concatenate([left, full, right], axis=-1)
    above = jnp.pad(wide[1][:, :-1], ((0, 0), (1, 0), (0, 0), (0, 0)))
    below = jnp.pad(wide[0][:, 1:], ((0, 0), (0, 1), (0, 0), (0, 0)))
    shifts = jnp.stack([above, wide[0], wide[1], below])
    shifts = shifts.reshape(4, frames, pairs_all * half, 4 * cout)

    taps = [conv_weight[:, :, tap_w] for tap_w in range(3)]
    blank = jnp.zeros_like(taps[0])
    big = jnp.concatenate(
        [
            jnp.concatenate([taps[2], taps[1], taps[0], blank], axis=-1),
            jnp.concatenate([blank, taps[2], taps[1], taps[0]], axis=-1),
        ],
        axis=2,
    )

    blocks = pairs_all // TILE
    span = TILE * half
    work = 2 * 9 * 3 * 2 * pairs_all * half * (2 * cin) * (4 * cout)
    x_block = pl.BlockSpec((4, frames, span, 4 * cout), lambda blk, tap: (0, 0, blk, 0))
    grad_out = pl.pallas_call(
        grad_out_kernel,
        grid=(blocks, 3),
        in_specs=[
            x_block,
            pl.BlockSpec((3, 1, 2 * cin, 4 * cout), lambda blk, tap: (0, tap, 0, 0)),
            pl.BlockSpec((count * depth, mine), lambda blk, tap: (0, 0)),
        ],
        out_specs=pl.BlockSpec((frames * span, mine), lambda blk, tap: (blk, 0)),
        out_shape=jax.ShapeDtypeStruct((length, mine), jnp.bfloat16),
        scratch_shapes=[pltpu.VMEM((2, frames * span, 2 * cin), jnp.float32)],
        compiler_params=pltpu.CompilerParams(vmem_limit_bytes=LIMIT),
        cost_estimate=flops(work, 20 << 20),
        name="grad_out",
    )(shifts, big, columns)

    step = max(1, 256 // tokens_here)
    head_block = pl.BlockSpec((count, 3, tokens_here, head_dim), lambda head: (0, 0, 0, head))
    heads_here = HEADS // count
    result = pl.pallas_call(
        lambda *refs: attention_kernel(step, *refs),
        grid=(heads_here,),
        in_specs=[head_block, pl.BlockSpec((length, head_dim), lambda head: (0, head))],
        out_specs=head_block,
        out_shape=jax.ShapeDtypeStruct((count, 3, tokens_here, mine), jnp.bfloat16),
        scratch_shapes=[pltpu.VMEM((length, head_dim), jnp.float32)] * 2,
        compiler_params=pltpu.CompilerParams(vmem_limit_bytes=LIMIT),
        cost_estimate=flops(heads_here * 20 * length * length * head_dim, 8 << 20),
        name="attention",
    )(moved, grad_out)

    shifts, result = lax.optimization_barrier((shifts, result))
    back = lax.all_to_all(result, "seq", split_axis=0, concat_axis=0, tiled=True)

    scale = 1.0 / math.sqrt(frames * rows_here * count * cols)
    shards = TILE // pairs
    weight_grad = pl.pallas_call(
        lambda *refs: weight_kernel(scale, blocks, *refs),
        grid=(3, blocks),
        in_specs=[
            pl.BlockSpec(
                (shards, 2, frames, pairs * half, 2 * cin), lambda tap, blk: (blk, 0, 0, 0, 0)
            ),
            pl.BlockSpec((4, frames, span, 4 * cout), lambda tap, blk: (0, 0, blk, 0)),
        ],
        out_specs=pl.BlockSpec((3, 1, 3, cin, cout), lambda tap, blk: (0, tap, 0, 0, 0)),
        out_shape=jax.ShapeDtypeStruct((3, 3, 3, cin, cout), jnp.float32),
        scratch_shapes=[pltpu.VMEM((2, 2 * cin, frames * span), jnp.bfloat16)],
        compiler_params=pltpu.CompilerParams(vmem_limit_bytes=LIMIT),
        cost_estimate=flops(work, 20 << 20),
        name="weight_grad",
    )(feat, shifts)
    back = back.transpose(1, 2, 0, 3).reshape(3, tokens_here, inner)
    return (weight_grad, back)


def fused_kernel(
    cot_ref, feat_ref, w_ref, map_ref, qkv_ref, wout_ref, back_ref,
    cot, feat, taps, big, cols, shifts, acc, grads, qkv_in, result, turned, dk, dv, stage,
    cot_send, cot_recv, feat_send, feat_recv, map_send, map_recv, share_send, share_recv,
    qkv_send, qkv_recv, back_send, back_recv, local, own, put,
):
    count = lax.axis_size("seq")
    parts = lax.axis_size("group")
    me = lax.axis_index("seq")
    member = lax.axis_index("group")
    lines = count // 2
    line, side_here = me // 2, lax.rem(me, 2)
    partner = me + 1 - 2 * side_here
    tokens, inner = qkv_ref.shape[1], qkv_ref.shape[2]
    mine = inner // count
    share = mine // parts
    depth = map_ref.shape[0]
    heads_here, head_dim = result.shape[0], result.shape[4]
    length = tokens * count
    frames, pairs_all, half = cot.shape[0], cot.shape[1], cot.shape[3]
    cout, cin = w_ref.shape[3], w_ref.shape[4]
    span = pairs_all * half
    each = pairs_all // count

    barrier = pltpu.get_barrier_semaphore()
    for hop in range(1, count):
        pl.semaphore_signal(
            barrier, inc=1, device_id={"seq": lax.rem(me + hop, count)}, device_id_type=MESH
        )
    for hop in range(1, parts):
        pl.semaphore_signal(
            barrier, inc=1, device_id={"group": lax.rem(member + hop, parts)}, device_id_type=MESH
        )
    pl.semaphore_wait(barrier, count + parts - 2)

    def send(src, dst, sent, got, target):
        return pltpu.make_async_remote_copy(
            src_ref=src, dst_ref=dst, send_sem=sent, recv_sem=got, device_id=target,
            device_id_type=MESH,
        )

    class Gather:
        def __init__(self, source, full, sent, got, done):
            self.source, self.full, self.sent, self.got, self.done = source, full, sent, got, done

        def rows(self, owner):
            return self.full.at[:, pl.ds(owner * each, each)]

        def copy(self, slot, owner, target, first=False):
            src = self.source if first else self.rows(owner)
            return send(
                src, self.rows(owner), self.sent.at[slot], self.got.at[owner], {"seq": target}
            )

        def moves(self, hop):
            if hop == 0:
                return (
                    (line + 1 < lines, 0, me, me + 2),
                    (line > 0, 1, me, me - 2),
                    (None, 2, me, partner),
                )
            low, high = me - 2 * hop, me + 2 * hop
            base = 4 * hop - 1
            has_low, has_high = line >= hop, line + hop < lines
            return (
                (has_low & (line + 1 < lines), base, low, me + 2),
                (has_high & (line > 0), base + 1, high, me - 2),
                (has_low, base + 2, low, partner),
                (has_high, base + 3, high, partner),
            )

        def step(self, hop):
            if hop == 0:
                self.keep().start()
            else:
                for valid, owner in (
                    (line >= hop, me - 2 * hop),
                    (line + hop < lines, me + 2 * hop),
                ):

                    @pl.when(valid)
                    def _():
                        self.copy(0, owner, partner).wait_recv()

            for valid, slot, owner, target in self.moves(hop):
                copy = self.copy(slot, owner, target, first=hop == 0)
                if valid is None:
                    copy.start()
                else:
                    pl.when(valid)(copy.start)

        def keep(self):
            return pltpu.make_async_copy(self.source, self.rows(me), self.done)

        def finish(self):
            for other in range(lines):
                self.copy(0, 2 * other + 1 - side_here, partner).wait_recv()
            self.keep().wait()

        def drain(self):
            for hop in range(lines):
                for valid, slot, owner, target in self.moves(hop):
                    copy = self.copy(slot, owner, target, first=hop == 0)
                    if valid is None:
                        copy.wait_send()
                    else:
                        pl.when(valid)(copy.wait_send)

    gather_cot = Gather(cot_ref, cot, cot_send, cot_recv, own.at[0])
    gather_feat = Gather(feat_ref, feat, feat_send, feat_recv, own.at[1])

    def map_piece(target):
        return map_ref.at[:, pl.ds(pl.multiple_of(target * mine + member * share, share), share)]

    def map_slot(owner):
        return cols.at[
            pl.ds(pl.multiple_of(owner * depth, depth), depth),
            pl.ds(pl.multiple_of(member * share, share), share),
        ]

    def map_copy(hop):
        target = lax.rem(me + hop, count)
        return send(
            map_piece(target), map_slot(me), map_send.at[hop - 1], map_recv.at[hop - 1], {"seq": target}
        )

    def share_copy(hop):
        block = cols.at[:, pl.ds(pl.multiple_of(member * share, share), share)]
        return send(
            block, block, share_send.at[hop - 1], share_recv.at[hop - 1],
            {"group": lax.rem(member + hop, parts)},
        )

    def qkv_copy(head, hop):
        target = lax.rem(me + hop, count)
        return send(
            qkv_ref.at[:, :, pl.ds(pl.multiple_of(target * mine + head * head_dim, head_dim), head_dim)],
            qkv_in.at[head, me],
            qkv_send.at[head, hop - 1],
            qkv_recv.at[head, hop - 1],
            {"seq": target},
        )

    def qkv_keep(head):
        return pltpu.make_async_copy(
            qkv_ref.at[:, :, pl.ds(pl.multiple_of(me * mine + head * head_dim, head_dim), head_dim)],
            qkv_in.at[head, me],
            local.at[head],
        )

    def back_copy(head, hop):
        target = lax.rem(me + hop, count)
        place = back_ref.at[
            :, :, pl.ds(pl.multiple_of(me * mine + head * head_dim, head_dim), head_dim)
        ]
        return send(
            result.at[head, target], place, back_send.at[head, hop - 1],
            back_recv.at[head, hop - 1], {"seq": target},
        )

    def back_keep(head):
        place = back_ref.at[
            :, :, pl.ds(pl.multiple_of(me * mine + head * head_dim, head_dim), head_dim)
        ]
        return pltpu.make_async_copy(result.at[head, me], place, local.at[head])

    map_keep = pltpu.make_async_copy(map_piece(me), map_slot(me), own.at[2])
    taps_in = pltpu.make_async_copy(w_ref, taps, own.at[3])

    gather_cot.step(0)
    for hop in range(1, count):
        map_copy(hop).start()
    taps_in.start()
    map_keep.start()
    for head in range(heads_here):
        qkv_keep(head).start()
    for hop in range(1, lines):
        gather_cot.step(hop)

    def start_head(head):
        for hop in range(1, count):
            qkv_copy(head, hop).start()

    gather_feat.step(0)
    start_head(0)
    for hop in range(1, count):
        map_copy(hop).wait_recv()
    map_keep.wait()
    for hop in range(1, parts):
        share_copy(hop).start()

    taps_in.wait()
    gather_cot.finish()

    row = lax.broadcasted_iota(jnp.int32, (span, 2 * cout), 0)
    lane = lax.broadcasted_iota(jnp.int32, (span, 2 * cout), 1)
    column = lax.rem(row, half)
    ahead = (lane < cout) & (column < half - 1)
    behind = (lane >= cout) & (column > 0)

    @pl.loop(0, 2 * frames)
    def _(index):
        side, frame = index // frames, lax.rem(index, frames)
        full = cot[frame, :, side].reshape(span, 2 * cout)
        value = full.astype(jnp.float32)
        above = pltpu.roll(value, span - 1, 0)
        below = pltpu.roll(value, 1, 0)
        rest = jnp.where(ahead, above, jnp.where(behind, below, 0.0)).astype(jnp.bfloat16)
        shifts[side + 1, frame, :, : 2 * cout] = full
        shifts[side + 1, frame, :, 2 * cout :] = rest
        both = jnp.concatenate([value, rest.astype(jnp.float32)], axis=1)
        place = jnp.where(side == 0, 3, 0)
        gap = jnp.zeros((half, 4 * cout), jnp.float32)
        down = jnp.concatenate([gap, both[: span - half]], axis=0)
        up = jnp.concatenate([both[half:], gap], axis=0)
        shifts[place, frame] = jnp.where(side == 0, up, down).astype(jnp.bfloat16)

    acc[...] = jnp.zeros_like(acc)

    def convolve(tap_h):
        blank = jnp.zeros((cout, cin), jnp.bfloat16)
        for tap_t in range(3):
            first, middle, last = (taps[tap_t, tap_h, tap_w] for tap_w in range(3))
            for column, pieces in enumerate(
                ((middle, first, blank, last), (last, middle, first, blank))
            ):
                for place, piece in enumerate(pieces):
                    big[
                        tap_t,
                        place * cout : (place + 1) * cout,
                        column * cin : (column + 1) * cin,
                    ] = piece

        @pl.loop(0, 2)
        def _(side):
            for tap_t in (2, 1, 0):
                live = frames - 2 + tap_t
                rows = shifts[side + 2 - tap_h, 2 - tap_t :].reshape(live * span, 4 * cout)
                acc[side, : live * span] += jnp.dot(
                    rows, big[tap_t], preferred_element_type=jnp.float32
                )

    @pl.loop(0, 3)
    def _(tap_h):
        convolve(tap_h)
        for hop in range(1, 4):

            @pl.when(tap_h == hop - 1)
            def _():
                gather_feat.step(hop)
                start_head(hop)

    for hop in range(1, parts):
        share_copy(hop).wait_recv()
    total = jnp.dot(
        acc[0].astype(jnp.bfloat16), cols[: 2 * cin], preferred_element_type=jnp.float32
    ) + jnp.dot(acc[1].astype(jnp.bfloat16), cols[2 * cin :], preferred_element_type=jnp.float32)
    total = total.reshape(frames, span // half, half, mine).transpose(1, 0, 2, 3)
    total = total.reshape(length, mine).astype(jnp.bfloat16)
    for head in range(heads_here):
        grads[head] = total[:, head * head_dim : (head + 1) * head_dim]

    step = max(1, 256 // tokens)

    @pl.loop(0, heads_here)
    def _(head):
        qkv_keep(head).wait()
        for hop in range(1, count):
            qkv_copy(head, hop).wait_recv()
        attention_kernel(step, qkv_in.at[head], grads.at[head], result.at[head], dk, dv)
        for hop in range(1, count):
            back_copy(head, hop).start()
        back_keep(head).start()

    gather_feat.finish()

    @pl.loop(0, 4)
    def _(index):
        for frame in range(frames):
            turned[index, :, frame * span : (frame + 1) * span] = shifts[index, frame].T

    scale = 1.0 / math.sqrt(2 * frames * span * 2)

    def out_copy(slot, tap_t, tap_h):
        return pltpu.make_async_copy(stage.at[slot, tap_t], wout_ref.at[tap_t, tap_h], put.at[slot, tap_t])

    @pl.loop(0, 3)
    def _(tap_h):
        slot = lax.rem(tap_h, 2)

        @pl.when(tap_h == 2)
        def _():
            for tap_t in range(3):
                out_copy(0, tap_t, 0).wait()

        for tap_t in range(3):
            live = frames - 2 + tap_t
            prod = None
            for side in range(2):
                rows = feat[:live, :, side].reshape(live * span, 2 * cin)
                part = jnp.dot(
                    turned[side + 2 - tap_h, :, (2 - tap_t) * span :],
                    rows,
                    preferred_element_type=jnp.float32,
                )
                prod = part if prod is None else prod + part
            even, odd = prod[:, :cin], prod[:, cin:]
            for tap_w, (low, high) in enumerate(((1, 2), (0, 1), (3, 0))):
                value = even[low * cout : (low + 1) * cout] + odd[high * cout : (high + 1) * cout]
                stage[slot, tap_t, tap_w] = value * scale
            out_copy(slot, tap_t, tap_h).start()

    for tap_t in range(3):
        out_copy(1, tap_t, 1).wait()
        out_copy(0, tap_t, 2).wait()

    gather_cot.drain()
    gather_feat.drain()
    for hop in range(1, count):
        map_copy(hop).wait_send()
    for hop in range(1, parts):
        share_copy(hop).wait_send()

    @pl.loop(0, heads_here)
    def _(head):
        for hop in range(1, count):
            qkv_copy(head, hop).wait_send()
            back_copy(head, hop).wait_send()
        for hop in range(1, count):
            back_copy(head, hop).wait_recv()
        back_keep(head).wait()


def per_device(features, cotangent, conv_weight, patch_map, qkv):
    frames, rows_here, cols, cin = features.shape
    cout = cotangent.shape[3]
    count, parts = lax.axis_size("seq"), lax.axis_size("group")
    half, pairs = cols // 2, rows_here // 2
    span = pairs * half * count
    tokens, inner = qkv.shape[1], qkv.shape[2]
    mine, head_dim = inner // count, inner // HEADS
    heads_here = HEADS // count
    depth = patch_map.shape[0]
    fits = count == 8 and heads_here == 4 and (mine // parts) % 128 == 0
    if not (fits and half == 8 and span == TILE * half):
        return per_device_general(features, cotangent, conv_weight, patch_map, qkv)

    def paired(value, wide):
        return value.reshape(frames, pairs, 2, half, 2 * wide)

    half_type, dma = jnp.bfloat16, pltpu.SemaphoreType.DMA
    whole = pl.BlockSpec(memory_space=pl.ANY)
    moves = 4 * (count // 2) - 1
    weight_grad, back = pl.pallas_call(
        fused_kernel,
        in_specs=[whole] * 5,
        out_specs=[whole] * 2,
        out_shape=[
            jax.ShapeDtypeStruct((3, 3, 3, cout, cin), jnp.float32),
            jax.ShapeDtypeStruct((3, tokens, inner), half_type),
        ],
        scratch_shapes=[
            pltpu.VMEM((frames, pairs * count, 2, half, 2 * cout), half_type),
            pltpu.VMEM((frames, pairs * count, 2, half, 2 * cin), half_type),
            pltpu.VMEM((3, 3, 3, cout, cin), half_type),
            pltpu.VMEM((3, 4 * cout, 2 * cin), half_type),
            pltpu.VMEM((count * depth, mine), half_type),
            pltpu.VMEM((4, frames, span, 4 * cout), half_type),
            pltpu.VMEM((2, frames * span, 2 * cin), jnp.float32),
            pltpu.VMEM((heads_here, tokens * count, head_dim), half_type),
            pltpu.VMEM((heads_here, count, 3, tokens, head_dim), half_type),
            pltpu.VMEM((heads_here, count, 3, tokens, head_dim), half_type),
            pltpu.VMEM((4, 4 * cout, frames * span), half_type),
            pltpu.VMEM((tokens * count, head_dim), jnp.float32),
            pltpu.VMEM((tokens * count, head_dim), jnp.float32),
            pltpu.VMEM((2, 3, 3, cout, cin), jnp.float32),
            dma((moves,)), dma((count,)), dma((moves,)), dma((count,)),
            dma((count - 1,)), dma((count - 1,)), dma((parts - 1,)), dma((parts - 1,)),
            dma((heads_here, count - 1)), dma((heads_here, count - 1)),
            dma((heads_here, count - 1)), dma((heads_here, count - 1)),
            dma((heads_here,)), dma((4,)), dma((2, 3)),
        ],
        compiler_params=pltpu.CompilerParams(
            collective_id=0, has_side_effects=True, vmem_limit_bytes=LIMIT
        ),
        name="fused",
    )(paired(cotangent, cout), paired(features, cin), conv_weight.swapaxes(3, 4), patch_map, qkv)
    return weight_grad.swapaxes(3, 4), back


def solution(mesh):
    placed = (
        P("group", "seq", None, None),
        P("group", "seq", None, None),
        P(),
        P("seq", None),
        P(None, ("group", "seq"), None),
    )
    return jax.shard_map(
        per_device,
        mesh=mesh,
        in_specs=placed,
        out_specs=(P("group", None, None, None, None), P(None, ("group", "seq"), None)),
        check_vma=False,
    )
```

```python
import math

import jax
import jax.numpy as jnp
from jax import lax
from jax.experimental import pallas as pl
from jax.experimental.pallas import tpu as pltpu
from jax.sharding import PartitionSpec as P

HEADS = 32
TILE = 32
LIMIT = 60 * 1024 * 1024
GRANT = 41 * 1024 * 1024
MESH = pl.DeviceIdType.MESH


def flops(count, moved):
    return pl.CostEstimate(flops=count, bytes_accessed=moved, transcendentals=0)


def grad_out_kernel(x_ref, w_ref, map_ref, out_ref, acc_ref):
    frames, span, wide = x_ref.shape[1], x_ref.shape[2], x_ref.shape[3]
    double = w_ref.shape[2]
    tap_h = pl.program_id(1)

    for side in range(2):
        for tap_t in (2, 1, 0):
            live = frames - 2 + tap_t
            rows = x_ref[side + 2 - tap_h, 2 - tap_t :].reshape(live * span, wide)
            part = lax.dot_general(
                rows, w_ref[tap_t, 0], (((1,), (1,)), ((), ())), preferred_element_type=jnp.float32
            )
            if tap_t == 2:

                @pl.when(tap_h == 0)
                def _():
                    acc_ref[side] = part

                @pl.when(tap_h > 0)
                def _():
                    acc_ref[side] += part

            else:
                acc_ref[side, : live * span] += part

    @pl.when(tap_h == 2)
    def _():
        wide_out = out_ref.shape[1]
        total = jnp.dot(
            acc_ref[0].astype(jnp.bfloat16), map_ref[:double], preferred_element_type=jnp.float32
        ) + jnp.dot(
            acc_ref[1].astype(jnp.bfloat16), map_ref[double:], preferred_element_type=jnp.float32
        )
        each = span // TILE
        total = total.reshape(frames, TILE, each, wide_out).transpose(1, 0, 2, 3)
        out_ref[...] = total.reshape(frames * span, wide_out).astype(jnp.bfloat16)


def weight_kernel(scale, blocks, feat_ref, x_ref, out_ref, turned_ref):
    frames, span, wide = x_ref.shape[1], x_ref.shape[2], x_ref.shape[3]
    double = feat_ref.shape[4]
    cin, cout = double // 2, wide // 4
    tap_h = pl.program_id(0)
    block = pl.program_id(1)

    def turn():
        for side in range(2):
            for frame in range(frames):
                turned_ref[side, :, frame * span : (frame + 1) * span] = (
                    feat_ref[:, side, frame].reshape(span, double).T
                )

    if blocks == 1:
        pl.when(tap_h == 0)(turn)
    else:
        turn()
    for tap_t in range(3):
        live = frames - 2 + tap_t
        prod = None
        for side in range(2):
            rows = x_ref[side + 2 - tap_h, 2 - tap_t :].reshape(live * span, wide)
            part = jnp.dot(
                turned_ref[side, :, : live * span], rows, preferred_element_type=jnp.float32
            )
            prod = part if prod is None else prod + part
        for tap_w in range(3):
            even = prod[:cin, cout * (2 - tap_w) : cout * (3 - tap_w)]
            odd = prod[cin:, cout * (3 - tap_w) : cout * (4 - tap_w)]
            value = (even + odd) * scale
            if blocks == 1:
                out_ref[tap_t, 0, tap_w] = value
            else:

                @pl.when(block == 0)
                def _():
                    out_ref[tap_t, 0, tap_w] = value

                @pl.when(block > 0)
                def _():
                    out_ref[tap_t, 0, tap_w] += value


def attention_kernel(step, qkv_ref, grad_ref, out_ref, dk_ref, dv_ref):
    shards, _, rows, width = qkv_ref.shape
    length = shards * rows
    scale = 1.0 / math.sqrt(width)
    keys = qkv_ref[:, 1].reshape(length, width)
    values = qkv_ref[:, 2].reshape(length, width)
    keys_t = keys.T
    span = step * rows

    def block(index, first):
        query = qkv_ref[pl.ds(index * step, step), 0].reshape(span, width)
        grads = grad_ref[pl.ds(pl.multiple_of(index * span, span), span), :]
        scores = lax.dot_general(
            keys, query, (((1,), (1,)), ((), ())), preferred_element_type=jnp.float32
        )
        top = jnp.max(scores, axis=0, keepdims=True)
        expo = jnp.exp((scores - top) * scale)
        probs = expo * (1.0 / jnp.sum(expo, axis=0, keepdims=True))
        dprob = lax.dot_general(
            values, grads, (((1,), (1,)), ((), ())), preferred_element_type=jnp.float32
        )
        delta = jnp.sum(probs * dprob, axis=0, keepdims=True)
        dscore = (probs * (dprob - delta)).astype(jnp.bfloat16)
        dquery = jnp.dot(keys_t, dscore, preferred_element_type=jnp.float32) * scale
        out_ref[pl.ds(index * step, step), 0] = (
            dquery.T.reshape(step, rows, width).astype(jnp.bfloat16)
        )
        part_k = jnp.dot(dscore, query, preferred_element_type=jnp.float32)
        part_v = jnp.dot(probs.astype(jnp.bfloat16), grads, preferred_element_type=jnp.float32)
        if first:
            dk_ref[...] = part_k
            dv_ref[...] = part_v
        else:
            dk_ref[...] += part_k
            dv_ref[...] += part_v

    count = shards // step
    if count <= 4:
        for index in range(count):
            block(index, index == 0)
    else:
        block(0, True)

        @pl.loop(1, count)
        def _(index):
            block(index, False)

    out_ref[:, 1] = (dk_ref[...] * scale).reshape(shards, rows, width).astype(jnp.bfloat16)
    out_ref[:, 2] = dv_ref[...].reshape(shards, rows, width).astype(jnp.bfloat16)


def per_device_general(features, cotangent, conv_weight, patch_map, qkv):
    frames, rows_here, cols, cin = features.shape
    cout = cotangent.shape[3]
    count = lax.axis_size("seq")
    parts = lax.axis_size("group")
    half, pairs = cols // 2, rows_here // 2
    pairs_all = pairs * count
    tokens_here, inner = qkv.shape[1], qkv.shape[2]
    length = tokens_here * count
    mine = inner // count
    head_dim = inner // HEADS

    cot = cotangent.reshape(frames, pairs, 2, half, 2 * cout).transpose(2, 0, 1, 3, 4)
    cot = lax.all_gather(cot.reshape(-1, 2 * cout), "seq", axis=0, tiled=True)
    sent = qkv.reshape(3, tokens_here, count, mine).transpose(2, 0, 1, 3)
    moved = lax.all_to_all(sent, "seq", split_axis=0, concat_axis=0, tiled=True)
    share = mine // parts
    depth = patch_map.shape[0]
    member = lax.axis_index("group")
    piece = lax.dynamic_index_in_dim(
        patch_map.reshape(depth, count, parts, share), member, axis=2, keepdims=False
    )
    piece = lax.all_to_all(
        piece.transpose(1, 0, 2), "seq", split_axis=0, concat_axis=0, tiled=True
    ).reshape(count * depth, share)
    columns = lax.all_gather(piece, "group", axis=0, tiled=False)
    columns = columns.transpose(1, 0, 2).reshape(count * depth, mine)
    feat = features.reshape(frames, pairs, 2, half, 2 * cin).transpose(2, 0, 1, 3, 4)
    feat = lax.all_gather(feat.reshape(-1, 2 * cin), "seq", axis=0, tiled=True)
    feat = feat.reshape(count, 2, frames, pairs * half, 2 * cin)

    full = cot.reshape(count, 2, frames, pairs, half, 2 * cout).transpose(1, 2, 0, 3, 4, 5)
    full = full.reshape(2, frames, pairs_all, half, 2 * cout)
    left = jnp.pad(full[:, :, :, :-1, cout:], ((0, 0), (0, 0), (0, 0), (1, 0), (0, 0)))
    right = jnp.pad(full[:, :, :, 1:, :cout], ((0, 0), (0, 0), (0, 0), (0, 1), (0, 0)))
    wide = jnp.concatenate([left, full, right], axis=-1)
    above = jnp.pad(wide[1][:, :-1], ((0, 0), (1, 0), (0, 0), (0, 0)))
    below = jnp.pad(wide[0][:, 1:], ((0, 0), (0, 1), (0, 0), (0, 0)))
    shifts = jnp.stack([above, wide[0], wide[1], below])
    shifts = shifts.reshape(4, frames, pairs_all * half, 4 * cout)

    taps = [conv_weight[:, :, tap_w] for tap_w in range(3)]
    blank = jnp.zeros_like(taps[0])
    big = jnp.concatenate(
        [
            jnp.concatenate([taps[2], taps[1], taps[0], blank], axis=-1),
            jnp.concatenate([blank, taps[2], taps[1], taps[0]], axis=-1),
        ],
        axis=2,
    )

    blocks = pairs_all // TILE
    span = TILE * half
    work = 2 * 9 * 3 * 2 * pairs_all * half * (2 * cin) * (4 * cout)
    x_block = pl.BlockSpec((4, frames, span, 4 * cout), lambda blk, tap: (0, 0, blk, 0))
    grad_out = pl.pallas_call(
        grad_out_kernel,
        grid=(blocks, 3),
        in_specs=[
            x_block,
            pl.BlockSpec((3, 1, 2 * cin, 4 * cout), lambda blk, tap: (0, tap, 0, 0)),
            pl.BlockSpec((count * depth, mine), lambda blk, tap: (0, 0)),
        ],
        out_specs=pl.BlockSpec((frames * span, mine), lambda blk, tap: (blk, 0)),
        out_shape=jax.ShapeDtypeStruct((length, mine), jnp.bfloat16),
        scratch_shapes=[pltpu.VMEM((2, frames * span, 2 * cin), jnp.float32)],
        compiler_params=pltpu.CompilerParams(vmem_limit_bytes=LIMIT),
        cost_estimate=flops(work, 20 << 20),
        name="grad_out",
    )(shifts, big, columns)

    step = max(1, 256 // tokens_here)
    head_block = pl.BlockSpec((count, 3, tokens_here, head_dim), lambda head: (0, 0, 0, head))
    heads_here = HEADS // count
    result = pl.pallas_call(
        lambda *refs: attention_kernel(step, *refs),
        grid=(heads_here,),
        in_specs=[head_block, pl.BlockSpec((length, head_dim), lambda head: (0, head))],
        out_specs=head_block,
        out_shape=jax.ShapeDtypeStruct((count, 3, tokens_here, mine), jnp.bfloat16),
        scratch_shapes=[pltpu.VMEM((length, head_dim), jnp.float32)] * 2,
        compiler_params=pltpu.CompilerParams(vmem_limit_bytes=LIMIT),
        cost_estimate=flops(heads_here * 20 * length * length * head_dim, 8 << 20),
        name="attention",
    )(moved, grad_out)

    shifts, result = lax.optimization_barrier((shifts, result))
    back = lax.all_to_all(result, "seq", split_axis=0, concat_axis=0, tiled=True)

    scale = 1.0 / math.sqrt(frames * rows_here * count * cols)
    shards = TILE // pairs
    weight_grad = pl.pallas_call(
        lambda *refs: weight_kernel(scale, blocks, *refs),
        grid=(3, blocks),
        in_specs=[
            pl.BlockSpec(
                (shards, 2, frames, pairs * half, 2 * cin), lambda tap, blk: (blk, 0, 0, 0, 0)
            ),
            pl.BlockSpec((4, frames, span, 4 * cout), lambda tap, blk: (0, 0, blk, 0)),
        ],
        out_specs=pl.BlockSpec((3, 1, 3, cin, cout), lambda tap, blk: (0, tap, 0, 0, 0)),
        out_shape=jax.ShapeDtypeStruct((3, 3, 3, cin, cout), jnp.float32),
        scratch_shapes=[pltpu.VMEM((2, 2 * cin, frames * span), jnp.bfloat16)],
        compiler_params=pltpu.CompilerParams(vmem_limit_bytes=LIMIT),
        cost_estimate=flops(work, 20 << 20),
        name="weight_grad",
    )(feat, shifts)
    back = back.transpose(1, 2, 0, 3).reshape(3, tokens_here, inner)
    return (weight_grad, back)


def fused_kernel(
    cot_ref, feat_ref, w_ref, map_ref, qkv_ref, wout_0, wout_1, wout_2, back_ref,
    cot, feat, taps, big, cols, shifts, acc, grads, qkv_in, result, turned, dk, dv, stage,
    cot_send, cot_recv, feat_send, feat_recv, map_send, map_recv, share_send, share_recv,
    qkv_send, qkv_recv, back_send, back_recv, local, own, put,
):
    count = lax.axis_size("seq")
    parts = lax.axis_size("group")
    me = lax.axis_index("seq")
    member = lax.axis_index("group")
    lines = count // 2
    line, side_here = me // 2, lax.rem(me, 2)
    partner = me + 1 - 2 * side_here
    tokens, inner = qkv_ref.shape[1], qkv_ref.shape[2]
    mine = inner // count
    share = mine // parts
    depth = map_ref.shape[0]
    heads_here, head_dim = result.shape[0], result.shape[4]
    length = tokens * count
    frames, pairs_all, half = cot.shape[0], cot.shape[1], cot.shape[3]
    cout, cin = w_ref.shape[3], w_ref.shape[4]
    span = pairs_all * half
    each = pairs_all // count

    barrier = pltpu.get_barrier_semaphore()
    for hop in range(1, count):
        pl.semaphore_signal(
            barrier, inc=1, device_id={"seq": lax.rem(me + hop, count)}, device_id_type=MESH
        )
    for hop in range(1, parts):
        pl.semaphore_signal(
            barrier, inc=1, device_id={"group": lax.rem(member + hop, parts)}, device_id_type=MESH
        )
    pl.semaphore_wait(barrier, count + parts - 2)

    def send(src, dst, sent, got, target):
        return pltpu.make_async_remote_copy(
            src_ref=src, dst_ref=dst, send_sem=sent, recv_sem=got, device_id=target,
            device_id_type=MESH,
        )

    class Gather:
        def __init__(self, source, full, sent, got, done):
            self.source, self.full, self.sent, self.got, self.done = source, full, sent, got, done

        def rows(self, owner):
            return self.full.at[:, pl.ds(owner * each, each)]

        def copy(self, slot, owner, target, first=False):
            src = self.source if first else self.rows(owner)
            return send(
                src, self.rows(owner), self.sent.at[slot], self.got.at[owner], {"seq": target}
            )

        def moves(self, hop):
            if hop == 0:
                return (
                    (line + 1 < lines, 0, me, me + 2),
                    (line > 0, 1, me, me - 2),
                    (None, 2, me, partner),
                )
            low, high = me - 2 * hop, me + 2 * hop
            base = 4 * hop - 1
            has_low, has_high = line >= hop, line + hop < lines
            return (
                (has_low & (line + 1 < lines), base, low, me + 2),
                (has_high & (line > 0), base + 1, high, me - 2),
                (has_low, base + 2, low, partner),
                (has_high, base + 3, high, partner),
            )

        def step(self, hop):
            if hop == 0:
                self.keep().start()
            else:
                for valid, owner in (
                    (line >= hop, me - 2 * hop),
                    (line + hop < lines, me + 2 * hop),
                ):

                    @pl.when(valid)
                    def _():
                        self.copy(0, owner, partner).wait_recv()

            for valid, slot, owner, target in self.moves(hop):
                copy = self.copy(slot, owner, target, first=hop == 0)
                if valid is None:
                    copy.start()
                else:
                    pl.when(valid)(copy.start)

        def keep(self):
            return pltpu.make_async_copy(self.source, self.rows(me), self.done)

        def finish(self):
            for other in range(lines):
                self.copy(0, 2 * other + 1 - side_here, partner).wait_recv()
            self.keep().wait()

        def drain(self):
            for hop in range(lines):
                for valid, slot, owner, target in self.moves(hop):
                    copy = self.copy(slot, owner, target, first=hop == 0)
                    if valid is None:
                        copy.wait_send()
                    else:
                        pl.when(valid)(copy.wait_send)

    gather_cot = Gather(cot_ref, cot, cot_send, cot_recv, own.at[0])
    gather_feat = Gather(feat_ref, feat, feat_send, feat_recv, own.at[1])

    def map_piece(target):
        return map_ref.at[:, pl.ds(pl.multiple_of(target * mine + member * share, share), share)]

    def map_slot(owner):
        return cols.at[
            pl.ds(pl.multiple_of(owner * depth, depth), depth),
            pl.ds(pl.multiple_of(member * share, share), share),
        ]

    def map_copy(hop):
        target = lax.rem(me + hop, count)
        return send(
            map_piece(target), map_slot(me), map_send.at[hop - 1], map_recv.at[hop - 1], {"seq": target}
        )

    def share_copy(hop):
        block = cols.at[:, pl.ds(pl.multiple_of(member * share, share), share)]
        return send(
            block, block, share_send.at[hop - 1], share_recv.at[hop - 1],
            {"group": lax.rem(member + hop, parts)},
        )

    def qkv_copy(head, hop):
        target = lax.rem(me + hop, count)
        return send(
            qkv_ref.at[:, :, pl.ds(pl.multiple_of(target * mine + head * head_dim, head_dim), head_dim)],
            qkv_in.at[head, me],
            qkv_send.at[head, hop - 1],
            qkv_recv.at[head, hop - 1],
            {"seq": target},
        )

    def qkv_keep(head):
        return pltpu.make_async_copy(
            qkv_ref.at[:, :, pl.ds(pl.multiple_of(me * mine + head * head_dim, head_dim), head_dim)],
            qkv_in.at[head, me],
            local.at[head],
        )

    def back_copy(head, hop):
        target = lax.rem(me + hop, count)
        place = back_ref.at[
            :, :, pl.ds(pl.multiple_of(me * mine + head * head_dim, head_dim), head_dim)
        ]
        return send(
            result.at[head, target], place, back_send.at[head, hop - 1],
            back_recv.at[head, hop - 1], {"seq": target},
        )

    def back_keep(head):
        place = back_ref.at[
            :, :, pl.ds(pl.multiple_of(me * mine + head * head_dim, head_dim), head_dim)
        ]
        return pltpu.make_async_copy(result.at[head, me], place, local.at[head])

    map_keep = pltpu.make_async_copy(map_piece(me), map_slot(me), own.at[2])

    def taps_in(tap_h):
        return pltpu.make_async_copy(w_ref.at[:, tap_h], taps, own.at[3])

    gather_cot.step(0)
    for hop in range(1, count):
        map_copy(hop).start()
    taps_in(0).start()
    map_keep.start()
    for head in range(heads_here):
        qkv_keep(head).start()
    for hop in range(1, lines):
        gather_cot.step(hop)

    def start_head(head):
        for hop in range(1, count):
            qkv_copy(head, hop).start()

    gather_feat.step(0)
    start_head(0)
    for hop in range(1, count):
        map_copy(hop).wait_recv()
    map_keep.wait()
    for hop in range(1, parts):
        share_copy(hop).start()

    gather_cot.finish()

    row = lax.broadcasted_iota(jnp.int32, (span, 2 * cout), 0)
    lane = lax.broadcasted_iota(jnp.int32, (span, 2 * cout), 1)
    column = lax.rem(row, half)
    ahead = (lane < cout) & (column < half - 1)
    behind = (lane >= cout) & (column > 0)

    @pl.loop(0, 2 * frames)
    def _(index):
        side, frame = index // frames, lax.rem(index, frames)
        full = cot[frame, :, side].reshape(span, 2 * cout)
        value = full.astype(jnp.float32)
        above = pltpu.roll(value, span - 1, 0)
        below = pltpu.roll(value, 1, 0)
        rest = jnp.where(ahead, above, jnp.where(behind, below, 0.0)).astype(jnp.bfloat16)
        shifts[side + 1, frame, :, : 2 * cout] = full
        shifts[side + 1, frame, :, 2 * cout :] = rest
        both = jnp.concatenate([value, rest.astype(jnp.float32)], axis=1)
        place = jnp.where(side == 0, 3, 0)
        gap = jnp.zeros((half, 4 * cout), jnp.float32)
        down = jnp.concatenate([gap, both[: span - half]], axis=0)
        up = jnp.concatenate([both[half:], gap], axis=0)
        shifts[place, frame] = jnp.where(side == 0, up, down).astype(jnp.bfloat16)

    acc[...] = jnp.zeros_like(acc)

    def convolve(tap_h):
        taps_in(tap_h).wait()
        blank = jnp.zeros((cout, cin), jnp.bfloat16)
        for tap_t in range(3):
            first, middle, last = (taps[tap_t, tap_w] for tap_w in range(3))
            for column, pieces in enumerate(
                ((middle, first, blank, last), (last, middle, first, blank))
            ):
                for place, piece in enumerate(pieces):
                    big[
                        tap_t,
                        place * cout : (place + 1) * cout,
                        column * cin : (column + 1) * cin,
                    ] = piece

        @pl.when(tap_h < 2)
        def _():
            taps_in(tap_h + 1).start()

        @pl.loop(0, 2)
        def _(side):
            for tap_t in (2, 1, 0):
                live = frames - 2 + tap_t
                rows = shifts[side + 2 - tap_h, 2 - tap_t :].reshape(live * span, 4 * cout)
                acc[side, : live * span] += jnp.dot(
                    rows, big[tap_t], preferred_element_type=jnp.float32
                )

    @pl.loop(0, 3)
    def _(tap_h):
        convolve(tap_h)
        for hop in range(1, 4):

            @pl.when(tap_h == hop - 1)
            def _():
                gather_feat.step(hop)
                start_head(hop)

    for hop in range(1, parts):
        share_copy(hop).wait_recv()
    total = jnp.dot(
        acc[0].astype(jnp.bfloat16), cols[: 2 * cin], preferred_element_type=jnp.float32
    ) + jnp.dot(acc[1].astype(jnp.bfloat16), cols[2 * cin :], preferred_element_type=jnp.float32)
    total = total.reshape(frames, span // half, half, mine).transpose(1, 0, 2, 3)
    total = total.reshape(length, mine).astype(jnp.bfloat16)
    for head in range(heads_here):
        grads[head] = total[:, head * head_dim : (head + 1) * head_dim]

    step = max(1, 256 // tokens)

    @pl.loop(0, heads_here)
    def _(head):
        qkv_keep(head).wait()
        for hop in range(1, count):
            qkv_copy(head, hop).wait_recv()
        attention_kernel(step, qkv_in.at[head], grads.at[head], result.at[head], dk, dv)
        for hop in range(1, count):
            back_copy(head, hop).start()
        back_keep(head).start()

    gather_feat.finish()

    scale = 1.0 / math.sqrt(2 * frames * span * 2)

    def out_copy(tap_t, tap_h):
        return pltpu.make_async_copy(
            stage.at[tap_t], (wout_0, wout_1, wout_2)[tap_t].at[tap_h], put.at[tap_t]
        )

    @pl.loop(0, 3)
    def _(tap_h):
        @pl.loop(0, 2)
        def _(side):
            for frame in range(frames):
                turned[side, :, frame * span : (frame + 1) * span] = (
                    shifts[side + 2 - tap_h, frame].T
                )

        for tap_t in range(3):
            live = frames - 2 + tap_t
            prod = None
            for side in range(2):
                rows = feat[:live, :, side].reshape(live * span, 2 * cin)
                part = jnp.dot(
                    turned[side, :, (2 - tap_t) * span :],
                    rows,
                    preferred_element_type=jnp.float32,
                )
                prod = part if prod is None else prod + part
            even, odd = prod[:, :cin], prod[:, cin:]

            @pl.when(tap_h > 0)
            def _():
                out_copy(tap_t, tap_h - 1).wait()

            for tap_w, (low, high) in enumerate(((1, 2), (0, 1), (3, 0))):
                value = even[low * cout : (low + 1) * cout] + odd[high * cout : (high + 1) * cout]
                stage[tap_t, tap_w] = value * scale
            out_copy(tap_t, tap_h).start()

    for tap_t in range(3):
        out_copy(tap_t, 2).wait()

    gather_cot.drain()
    gather_feat.drain()
    for hop in range(1, count):
        map_copy(hop).wait_send()
    for hop in range(1, parts):
        share_copy(hop).wait_send()

    @pl.loop(0, heads_here)
    def _(head):
        for hop in range(1, count):
            qkv_copy(head, hop).wait_send()
            back_copy(head, hop).wait_send()
        for hop in range(1, count):
            back_copy(head, hop).wait_recv()
        back_keep(head).wait()


def place_kernel(part_0, part_1, part_2, rows, weight_grad, back, done):
    copies = [
        pltpu.make_async_copy(part, weight_grad.at[tap], done.at[tap])
        for tap, part in enumerate((part_0, part_1, part_2))
    ]
    copies += [
        pltpu.make_async_copy(rows.at[which], back.at[which], done.at[3 + which])
        for which in range(3)
    ]
    for copy in copies:
        copy.start()
    for copy in copies:
        copy.wait()


def per_device(features, cotangent, conv_weight, patch_map, qkv):
    frames, rows_here, cols, cin = features.shape
    cout = cotangent.shape[3]
    count, parts = lax.axis_size("seq"), lax.axis_size("group")
    half, pairs = cols // 2, rows_here // 2
    span = pairs * half * count
    tokens, inner = qkv.shape[1], qkv.shape[2]
    mine, head_dim = inner // count, inner // HEADS
    heads_here = HEADS // count
    depth = patch_map.shape[0]
    fits = count == 8 and heads_here == 4 and (mine // parts) % 128 == 0
    if not (fits and half == 8 and span == TILE * half):
        return per_device_general(features, cotangent, conv_weight, patch_map, qkv)

    def paired(value, wide):
        return value.reshape(frames, pairs, 2, half, 2 * wide)

    half_type, dma = jnp.bfloat16, pltpu.SemaphoreType.DMA
    whole = pl.BlockSpec(memory_space=pl.ANY)
    moves = 4 * (count // 2) - 1
    *weight_grad, back = pl.pallas_call(
        fused_kernel,
        in_specs=[whole] * 5,
        out_specs=[whole] * 4,
        out_shape=[
            *[jax.ShapeDtypeStruct((3, 3, cout, cin), jnp.float32)] * 3,
            jax.ShapeDtypeStruct((3, tokens, inner), half_type),
        ],
        scratch_shapes=[
            pltpu.VMEM((frames, pairs * count, 2, half, 2 * cout), half_type),
            pltpu.VMEM((frames, pairs * count, 2, half, 2 * cin), half_type),
            pltpu.VMEM((3, 3, cout, cin), half_type),
            pltpu.VMEM((3, 4 * cout, 2 * cin), half_type),
            pltpu.VMEM((count * depth, mine), half_type),
            pltpu.VMEM((4, frames, span, 4 * cout), half_type),
            pltpu.VMEM((2, frames * span, 2 * cin), jnp.float32),
            pltpu.VMEM((heads_here, tokens * count, head_dim), half_type),
            pltpu.VMEM((heads_here, count, 3, tokens, head_dim), half_type),
            pltpu.VMEM((heads_here, count, 3, tokens, head_dim), half_type),
            pltpu.VMEM((2, 4 * cout, frames * span), half_type),
            pltpu.VMEM((tokens * count, head_dim), jnp.float32),
            pltpu.VMEM((tokens * count, head_dim), jnp.float32),
            pltpu.VMEM((3, 3, cout, cin), jnp.float32),
            dma((moves,)), dma((count,)), dma((moves,)), dma((count,)),
            dma((count - 1,)), dma((count - 1,)), dma((parts - 1,)), dma((parts - 1,)),
            dma((heads_here, count - 1)), dma((heads_here, count - 1)),
            dma((heads_here, count - 1)), dma((heads_here, count - 1)),
            dma((heads_here,)), dma((4,)), dma((3,)),
        ],
        compiler_params=pltpu.CompilerParams(
            collective_id=0, has_side_effects=True, vmem_limit_bytes=GRANT
        ),
        name="fused",
    )(paired(cotangent, cout), paired(features, cin), conv_weight.swapaxes(3, 4), patch_map, qkv)
    weight_grad, back = pl.pallas_call(
        place_kernel,
        in_specs=[whole] * 4,
        out_specs=[whole] * 2,
        out_shape=[
            jax.ShapeDtypeStruct((3, 3, 3, cout, cin), jnp.float32),
            jax.ShapeDtypeStruct((3, tokens, inner), half_type),
        ],
        scratch_shapes=[dma((6,))],
        compiler_params=pltpu.CompilerParams(vmem_limit_bytes=1 << 20),
        name="place",
    )(*weight_grad, back)
    return weight_grad.swapaxes(3, 4), back


def solution(mesh):
    placed = (
        P("group", "seq", None, None),
        P("group", "seq", None, None),
        P(),
        P("seq", None),
        P(None, ("group", "seq"), None),
    )
    return jax.shard_map(
        per_device,
        mesh=mesh,
        in_specs=placed,
        out_specs=(P("group", None, None, None, None), P(None, ("group", "seq"), None)),
        check_vma=False,
    )
```
